32 devices in a mesh: level: 4 (over x, core), gx: 2 (over y), gy: 4 (over z).
Axes of the slice: x: 2, y: 2, z: 4, core: 2. Of those that a mesh axis runs over, the one named last changes fastest.
Arguments:
- initial: float32 [8, 128, 512], P('gx', 'gy'), may hold values from -1 to 1
- mobility: float32 [8, 128, 512], P('gx', 'gy'), may hold values from 0.5 to 1.5
Outputs:
- finals: float32 [4, 8, 128, 512], P('level', 'gx', 'gy')
The draws below stay inside these ranges and needn't reach their ends.
All inputs are finite; a program needn't handle non-finite values.
Results may differ from the reference program's by a relative error of at most 0.00002.
Values sent between devices are 32-bit elements; how exact they have to be, the bound alone decides.
A program may use at most 64 MiB of HBM per device.

```python
import math
import jax
import jax.numpy as jnp

STEPS = 5
LEVELS = 4
NX = 8
NY = 128
NZ = 512


def block_scale(key, extent, split, low, high):
    factor_of, own = 1.0, jax.random.fold_in(key, 6)
    for dim, parts in split:
        steps = jnp.exp(jax.random.uniform(jax.random.fold_in(own, dim), (parts,), jnp.float32, low / len(split), high / len(split)))
        factor_of = factor_of * jnp.repeat(steps, extent[dim] // parts).reshape([-1 if axis == dim else 1 for axis in range(len(extent))])
    return factor_of


def setup_inputs(seed: int = 0) -> dict:
    arg_keys = jax.random.split(jax.random.key(seed), 3)
    return {
        "initial": jnp.clip(jax.random.uniform(arg_keys[0], (NX, NY, NZ), jnp.float32, -1.0, 1.0) * block_scale(arg_keys[0], (NX, NY, NZ), ((0, 2), (1, 4)), -0.4, 0.0), -1.0, 1.0),
        "mobility": jnp.clip(jnp.exp(math.log(1.5) - 1.0986123 * jax.random.uniform(arg_keys[1], (NX, NY, NZ), jnp.float32) ** block_scale(arg_keys[1], (NX, NY, NZ), ((0, 2), (1, 4)), -0.2, 0.2)), 0.5, 1.5),
    }


time_step = 0.004
gradient_energy = 1.0


def basis_integral(member, count_points, start_point, end_point):
    poly_terms = [1.0]
    denominator = 1.0
    for partner in range(count_points):
        if partner != member:
            widened = [0.0] * (len(poly_terms) + 1)
            for degree in range(len(poly_terms)):
                widened[degree + 1] += poly_terms[degree]
                widened[degree] -= partner * poly_terms[degree]
            poly_terms = widened
            denominator = denominator * (member - partner)
    integral = 0.0
    for degree in range(len(poly_terms)):
        integral += poly_terms[degree] * (end_point ** (degree + 1) - start_point ** (degree + 1)) / (degree + 1)
    return integral / denominator


def quadrature_rows(count_steps):
    weights = [[0.0] * (count_steps + 1) for interval in range(count_steps)]
    for interval in range(count_steps):
        for member in range(interval + 2):
            weights[interval][member] = basis_integral(member, interval + 2, 1.0 * interval, 1.0 * interval + 1.0)
        weights[interval][interval] -= 1.0
    return weights


def tendency(concentration, mobility):
    laplace = -6.0 * concentration
    for axis_id in range(3):
        laplace = laplace + jnp.roll(concentration, 1, axis_id) + jnp.roll(concentration, -1, axis_id)
    potential = concentration * concentration * concentration - concentration - gradient_energy * laplace
    result = jnp.zeros_like(concentration)
    for axis_id in range(3):
        face_mobility = 0.5 * (mobility + jnp.roll(mobility, -1, axis_id))
        face_flux = face_mobility * (jnp.roll(potential, -1, axis_id) - potential)
        result = result + face_flux - jnp.roll(face_flux, 1, axis_id)
    return result


def reference(initial, mobility):
    coefficient_rows = quadrature_rows(STEPS)
    previous = None
    finals = []
    for level_id in range(LEVELS):
        solution = initial
        history = []
        for interval in range(STEPS):
            current = tendency(solution, mobility)
            history.append(current)
            if previous is None:
                solution = solution + time_step * current
            else:
                correction = jnp.zeros_like(solution)
                for member in range(interval + 2):
                    correction = correction + jnp.float32(coefficient_rows[interval][member]) * previous[member]
                solution = solution + time_step * (current + correction)
        history.append(tendency(solution, mobility))
        previous = history
        finals.append(solution)
    return jnp.stack(finals)
```

```python
import functools

import jax
import jax.numpy as jnp
from jax import lax
from jax.experimental import pallas as pl
from jax.experimental.pallas import tpu as pltpu
from jax.sharding import PartitionSpec as P

STEPS = 5


time_step = 0.004
gradient_energy = 1.0


def padded_2(cells, sides, width):
    for axis, dim in sides:
        count = lax.axis_size(axis)
        head = lax.slice_in_dim(cells, 0, width, axis=dim)
        tail = lax.slice_in_dim(cells, cells.shape[dim] - width, cells.shape[dim], axis=dim)
        cells = jnp.concatenate(
            [
                lax.ppermute(tail, axis, [(i, (i + 1) % count) for i in range(count)]),
                cells,
                lax.ppermute(head, axis, [((i + 1) % count, i) for i in range(count)]),
            ],
            axis=dim,
        )
    return cells


def passed_along(shard, axis, by):
    count = lax.axis_size(axis)
    pairs = [(i, i + by) for i in range(count) if 0 <= i + by < count]
    return lax.ppermute(shard, axis, pairs)


def basis_integral(member, count_points, start_point, end_point):
    poly_terms = [1.0]
    denominator = 1.0
    for partner in range(count_points):
        if partner != member:
            widened = [0.0] * (len(poly_terms) + 1)
            for degree in range(len(poly_terms)):
                widened[degree + 1] += poly_terms[degree]
                widened[degree] -= partner * poly_terms[degree]
            poly_terms = widened
            denominator = denominator * (member - partner)
    integral = 0.0
    for degree in range(len(poly_terms)):
        integral += (
            poly_terms[degree]
            * (end_point ** (degree + 1) - start_point ** (degree + 1))
            / (degree + 1)
        )
    return integral / denominator


def quadrature_rows(count_steps):
    weights = [[0.0] * (count_steps + 1) for interval in range(count_steps)]
    for interval in range(count_steps):
        for member in range(interval + 2):
            weights[interval][member] = basis_integral(
                member, interval + 2, 1.0 * interval, 1.0 * interval + 1.0
            )
        weights[interval][interval] -= 1.0
    return weights


def extend(concentration):
    return padded_2(concentration, (("gx", 0), ("gy", 1)), 2)


def face_table(mobility):
    padded = padded_2(mobility, (("gx", 0), ("gy", 1)), 1)
    centre = padded[1:-1, 1:-1]
    x_plus = 0.5 * (centre + padded[2:, 1:-1])
    x_minus = 0.5 * (centre + padded[:-2, 1:-1])
    y_plus = 0.5 * (centre + padded[1:-1, 2:])
    y_minus = 0.5 * (centre + padded[1:-1, :-2])
    z_plus = 0.5 * (centre + jnp.roll(centre, -1, 2))
    z_minus = 0.5 * (centre + jnp.roll(centre, 1, 2))
    return (x_plus, x_minus, y_plus, y_minus, z_plus, z_minus)


def tendency_local(padded, faces):
    centre = padded[1:-1, 1:-1]
    laplace = -6.0 * centre
    laplace = laplace + padded[2:, 1:-1] + padded[:-2, 1:-1]
    laplace = laplace + padded[1:-1, 2:] + padded[1:-1, :-2]
    laplace = laplace + jnp.roll(centre, 1, 2) + jnp.roll(centre, -1, 2)
    potential = centre * centre * centre - centre - gradient_energy * laplace
    inner = potential[1:-1, 1:-1]
    result = faces[0] * (potential[2:, 1:-1] - inner) - faces[1] * (inner - potential[:-2, 1:-1])
    result = (
        result
        + faces[2] * (potential[1:-1, 2:] - inner)
        - faces[3] * (inner - potential[1:-1, :-2])
    )
    result = (
        result
        + faces[4] * (jnp.roll(inner, -1, 2) - inner)
        - faces[5] * (inner - jnp.roll(inner, 1, 2))
    )
    return result


def weighted_sum(weight_row, history):
    total = jnp.zeros(history.shape[1:], jnp.float32)
    for member in range(history.shape[0]):
        total = total + weight_row[member] * history[member]
    return total


def body(initial, mobility):
    level_count = lax.axis_size("level")
    level_id = lax.axis_index("level")
    faces = face_table(mobility)
    coefficients = jnp.asarray(quadrature_rows(STEPS), jnp.float32)
    node_ids = jnp.arange(STEPS + 1, dtype=jnp.int32)[:, None, None, None]
    solution = initial
    history = jnp.zeros((STEPS + 1,) + initial.shape, jnp.float32)
    for wave in range(STEPS + level_count - 1):
        interval = wave - level_id
        current = tendency_local(extend(solution), faces)
        arrived = passed_along(current, "level", 1)
        history = jnp.where(node_ids == interval + 1, arrived[None], history)
        weight_row = coefficients[jnp.clip(interval, 0, STEPS - 1)]
        correction = weighted_sum(weight_row, history)
        correction = jnp.where(level_id > 0, correction, jnp.zeros_like(correction))
        stepped = solution + time_step * (current + correction)
        active = jnp.logical_and(interval >= 0, interval < STEPS)
        solution = jnp.where(active, stepped, solution)
    return solution[None]


def window_kernel(weights, c_ref, m_ref, out_ref, raw, c0, mx, my, mz, rates_a, rates_b, sol_a, sol_b,
                  ready, finals, send_sem, recv_sem, fwd_send_sem, fwd_recv_sem, own_sem,
                  fin_send_sem, fin_recv_sem, fin_own_sem):
    steps = len(weights)
    level = lax.axis_index("level")
    gx = lax.axis_index("gx")
    gy = lax.axis_index("gy")
    count_y = lax.axis_size("gy")
    x = level // 2
    core = level % 2
    tile = 2 * gx + x
    above = lax.rem(gy + 1, count_y)
    below = lax.rem(gy + count_y - 1, count_y)
    mesh_type = pl.DeviceIdType.MESH

    barrier = pltpu.get_barrier_semaphore()
    greeted = [(level + 1 - 2 * core, gx, gy)]
    greeted += [(2 * (1 - x) + core, gx, gy), (2 * (1 - x) + core, 1 - gx, gy), (level, 1 - gx, gy)]
    greeted += [(level, side, other) for side in (gx, 1 - gx) for other in (above, below)]
    for device in greeted:
        pl.semaphore_signal(barrier, inc=1, device_id=device, device_id_type=mesh_type)
    pl.semaphore_wait(barrier, len(greeted))

    def aligned(row):
        return pl.multiple_of(row, 8)

    def region(array, half, row, count):
        return raw.at[array, pl.ds(4 * half, 4), pl.ds(aligned(row), count), :]

    def outgoing(array, source):
        partner_tile = 2 * (1 - gx) + x
        low = jnp.where(partner_tile == 3, 1, 0)

        def piece(row, count):
            return source.at[:, pl.ds(aligned(row), count), :]

        def copy(src, dst, slot, kind, device):
            return pltpu.make_async_remote_copy(
                src_ref=src, dst_ref=dst, send_sem=send_sem.at[slot], recv_sem=recv_sem.at[kind],
                device_id=device, device_id_type=mesh_type)

        to_above = (level, 0, above)
        to_below = (level, 1, below)
        partner = (level, 1 - gx, gy)
        row_to = 8 * jnp.maximum(2 - partner_tile, 0)
        return [
            (None, copy(piece(8 * low, 24), region(array, gx, row_to, 24), 0, 0, partner)),
            (x == gx, copy(piece(24, 8), region(array, gx, jnp.where(x == gx, 8 * (5 - partner_tile), 0), 8), 1, 1, partner)),
            (x == 0, copy(piece(16, 16), region(array, gx, 0, 16), 2, 2 + gx, to_above)),
            (x == 1, copy(piece(24, 8), region(array, gx, 0, 8), 2, 2 + gx, to_above)),
            (x == 1, copy(piece(0, 16), region(array, gx, 24, 16), 3, 3 - gx, to_below)),
            (x == 0, copy(piece(0, 8), region(array, gx, 32, 8), 3, 3 - gx, to_below)),
        ]

    def when(condition, action):
        if condition is None:
            action()
        else:
            pl.when(condition)(action)

    sibling = (level + 1 - 2 * core, gx, gy)

    def arriving(array):
        def copy(half, row, count, kind):
            where = region(array, half, row, count)
            landed = pltpu.make_async_remote_copy(
                src_ref=where, dst_ref=where, send_sem=send_sem.at[0], recv_sem=recv_sem.at[kind],
                device_id=sibling, device_id_type=mesh_type)
            handed = pltpu.make_async_remote_copy(
                src_ref=where, dst_ref=where, send_sem=fwd_send_sem.at[kind],
                recv_sem=fwd_recv_sem.at[kind], device_id=sibling, device_id_type=mesh_type)
            return landed, handed

        same = x == gx
        entries = [
            (None, copy(1 - gx, 8 * jnp.maximum(2 - tile, 0), 24, 0)),
            (jnp.logical_not(same), copy(1 - gx, jnp.where(same, 0, 8 * (5 - tile)), 8, 1)),
        ]
        for half, kind in ((gx, 2), (1 - gx, 3)):
            entries.append((same, copy(half, 24 * gx, 16, kind)))
            entries.append((jnp.logical_not(same), copy(half, 32 * gx, 8, kind)))
        return entries

    def own(array, source):
        low = jnp.where(tile == 3, 1, 0)
        row_to = 8 * jnp.maximum(2 - tile, 0)
        return [
            (None, pltpu.make_async_copy(
                source.at[:, pl.ds(aligned(8 * low), 24), :], region(array, gx, row_to, 24), own_sem.at[array, 0])),
            (x != gx, pltpu.make_async_copy(
                source.at[:, pl.ds(24, 8), :], region(array, gx, jnp.where(x != gx, 8 * (5 - tile), 0), 8),
                own_sem.at[array, 1])),
        ]

    for array, source in enumerate((c_ref, m_ref)):
        @pl.when(core == array)
        def _(array=array, source=source):
            for condition, copy in outgoing(array, source):
                when(condition, copy.start)
    for array, source in enumerate((c_ref, m_ref)):
        for condition, copy in own(array, source):
            when(condition, copy.start)
    for array in range(2):
        @pl.when(core == array)
        def _(array=array):
            for condition, (landed, handed) in arriving(array):
                def pass_on(landed=landed, handed=handed):
                    landed.wait_recv()
                    handed.start()
                when(condition, pass_on)
    for array, source in enumerate((c_ref, m_ref)):
        for condition, copy in own(array, source):
            when(condition, copy.wait)
    for array, source in enumerate((c_ref, m_ref)):
        @pl.when(core == array)
        def _(array=array, source=source):
            for condition, copy in outgoing(array, source):
                when(condition, copy.wait_send)
            for condition, (landed, handed) in arriving(array):
                when(condition, handed.wait_send)
            for condition, (landed, handed) in arriving(1 - array):
                when(condition, handed.wait_recv)

    width = c_ref.shape[2]

    def roll_x(cells, by):
        return pltpu.roll(cells, by % 8, 0)

    def roll_z(cells, by):
        return pltpu.roll(cells, by % width, 1)

    def turn(block, carry):
        row = pl.multiple_of(8 * block, 8)
        for array, target in ((0, c0), (1, sol_a)):
            for lane in range(0, width, 128):
                cells = raw[array, :, pl.ds(row, 8), lane:lane + 128]
                target[pl.ds(row, 8), :, lane:lane + 128] = jnp.swapaxes(cells, 0, 1)
        return carry

    lax.fori_loop(0, 5, turn, 0)

    half_step = 0.5 * time_step

    def faces(row, carry):
        here = sol_a[row]
        mx[row] = half_step * (here + roll_x(here, -1))
        mz[row] = half_step * (here + roll_z(here, -1))
        my[row] = half_step * (here + sol_a[row + 1])
        return carry

    lax.fori_loop(1, 39, faces, 0)

    def potential(state, row):
        centre = state[row]
        around = state[row - 1] + state[row + 1]
        around = around + (roll_x(centre, 1) + roll_x(centre, -1))
        around = around + (roll_z(centre, 1) + roll_z(centre, -1))
        return (centre * centre + (6.0 * gradient_energy - 1.0)) * centre - gradient_energy * around

    def evaluate(state, reach, rates_out, update):
        first, last = 16 - reach, 24 + reach
        here = potential(state, first)
        flux = my[first - 1] * (here - potential(state, first - 1))

        def group(index, carry):
            here, flux = carry
            for offset in range(4):
                row = first + 4 * index + offset
                after = potential(state, row + 1)
                flux_after = my[row] * (after - here)
                flux_x = mx[row] * (roll_x(here, -1) - here)
                flux_z = mz[row] * (roll_z(here, -1) - here)
                rate = flux_after - flux
                rate = rate + (flux_x - roll_x(flux_x, 1))
                rate = rate + (flux_z - roll_z(flux_z, 1))
                if rates_out is not None:
                    rates_out[row] = rate
                if update is not None:
                    update(row, rate)
                here, flux = after, flux_after
            return here, flux

        lax.fori_loop(0, (last - first) // 4, group, (here, flux))

    def deliveries(slot):
        result = []
        into = finals.at[:, pl.ds(aligned(8 * tile), 8), :]
        for to_x, to_gx in ((slot, 0), (slot, 1)):
            stays = jnp.logical_and(x == to_x, gx == to_gx)
            out = ready.at[slot, pl.ds(4 * to_gx, 4)]
            remote = pltpu.make_async_remote_copy(
                src_ref=out, dst_ref=into, send_sem=fin_send_sem.at[2 * slot + to_gx],
                recv_sem=fin_recv_sem.at[tile], device_id=(2 * to_x + core, to_gx, gy),
                device_id_type=mesh_type)
            local = pltpu.make_async_copy(out, into, fin_own_sem)
            result.append((pl.when(jnp.logical_not(stays)), remote, pl.when(stays), local))
        return result

    def send_out(slot, state):
        for lane in range(0, width, 128):
            ready[slot, :, :, lane:lane + 128] = jnp.swapaxes(state[16:24, :, lane:lane + 128], 0, 1)
        for goes, remote, stays, local in deliveries(slot):
            goes(remote.start)
            stays(local.start)

    first_reach = 2 * (steps + 2)

    def run_level(index):
        below_rates = (rates_a, rates_b)[(index + 1) % 2]
        own_rates = (rates_a, rates_b)[index % 2]
        states = (sol_a, sol_b)

        def below_rate(node, row):
            return rates_a[0, row] if node == 0 else below_rates[node, row]

        def corrected(interval, row, base, rate):
            total = rate
            if index > 0:
                for node in range(interval + 2):
                    factor = weights[interval][node]
                    if interval == 0 and node == 0:
                        factor = factor + 1.0
                        total = factor * below_rate(0, row)
                    else:
                        total = total + factor * below_rate(node, row)
            return base + total

        for interval in range(steps + 1):
            reach = first_reach - 2 * (index + interval)
            source = c0 if interval == 0 else states[interval % 2]
            target = states[(interval + 1) % 2]

            def update(row, rate, interval=interval, source=source, target=target):
                target[row] = corrected(interval, row, source[row], rate)

            if interval == 0 and index > 0:
                def start(group, carry, update=update, reach=reach):
                    for offset in range(4):
                        update(16 - reach + 4 * group + offset, None)
                    return carry
                lax.fori_loop(0, (8 + 2 * reach) // 4, start, 0)
            elif interval < steps:
                evaluate(source, reach, own_rates.at[interval] if index < 3 else None, update)
            elif index < 3:
                evaluate(source, reach, own_rates.at[interval], None)
            if interval == steps - 1:
                @pl.when(core == index % 2)
                def _(target=target):
                    send_out(index // 2, target)

    for index in range(3):
        run_level(index)
    pl.when(core == 1)(lambda: run_level(3))

    for slot in range(2):
        for goes, remote, stays, local in deliveries(slot):
            goes(remote.wait_send)
            stays(local.wait)
    for source_tile in range(4):
        into = finals.at[:, pl.ds(8 * source_tile, 8), :]
        arrived = pltpu.make_async_remote_copy(
            src_ref=into, dst_ref=into, send_sem=fin_send_sem.at[0],
            recv_sem=fin_recv_sem.at[source_tile], device_id=sibling, device_id_type=mesh_type)
        pl.when(tile != source_tile)(arrived.wait_recv)
    out_ref[0] = finals[...]


def window_body(initial, mobility):
    f32 = jnp.float32
    width = initial.shape[2]
    weights = quadrature_rows(STEPS)
    field = pltpu.VMEM((40, 8, width), f32)
    return pl.pallas_call(
        functools.partial(window_kernel, weights),
        out_shape=jax.ShapeDtypeStruct((1,) + initial.shape, f32),
        in_specs=[pl.BlockSpec(memory_space=pltpu.VMEM)] * 2,
        out_specs=pl.BlockSpec(memory_space=pltpu.VMEM),
        scratch_shapes=[
            pltpu.VMEM((2, 8, 40, width), f32),
            field, field, field, field,
            pltpu.VMEM((STEPS + 1, 40, 8, width), f32),
            pltpu.VMEM((STEPS + 1, 40, 8, width), f32),
            field, field,
            pltpu.VMEM((2, 8, 8, width), f32),
            pltpu.VMEM(initial.shape, f32),
            pltpu.SemaphoreType.DMA((4,)),
            pltpu.SemaphoreType.DMA((4,)),
            pltpu.SemaphoreType.DMA((4,)),
            pltpu.SemaphoreType.DMA((4,)),
            pltpu.SemaphoreType.DMA((2, 2)),
            pltpu.SemaphoreType.DMA((4,)),
            pltpu.SemaphoreType.DMA((4,)),
            pltpu.SemaphoreType.DMA,
        ],
        compiler_params=pltpu.CompilerParams(
            collective_id=0, has_side_effects=True, vmem_limit_bytes=40 * 1024 * 1024
        ),
    )(initial, mobility)


def solution(mesh):
    placed = (P("gx", "gy", None), P("gx", "gy", None))

    def chosen(initial, mobility):
        sizes = mesh.shape
        whole = (sizes["level"], sizes["gx"]) == (4, 2) and initial.shape[:2] == (4, 32)
        if whole and sizes["gy"] > 1 and initial.shape[2] % 128 == 0:
            return window_body(initial, mobility)
        return body(initial, mobility)

    return jax.shard_map(
        chosen, mesh=mesh, in_specs=placed, out_specs=P("level", "gx", "gy", None), check_vma=False
    )
```

```python
import functools

import jax
import jax.numpy as jnp
from jax import lax
from jax.experimental import pallas as pl
from jax.experimental.pallas import tpu as pltpu
from jax.sharding import PartitionSpec as P

STEPS = 5


time_step = 0.004
gradient_energy = 1.0


def padded_2(cells, sides, width):
    for axis, dim in sides:
        count = lax.axis_size(axis)
        head = lax.slice_in_dim(cells, 0, width, axis=dim)
        tail = lax.slice_in_dim(cells, cells.shape[dim] - width, cells.shape[dim], axis=dim)
        cells = jnp.concatenate(
            [
                lax.ppermute(tail, axis, [(i, (i + 1) % count) for i in range(count)]),
                cells,
                lax.ppermute(head, axis, [((i + 1) % count, i) for i in range(count)]),
            ],
            axis=dim,
        )
    return cells


def passed_along(shard, axis, by):
    count = lax.axis_size(axis)
    pairs = [(i, i + by) for i in range(count) if 0 <= i + by < count]
    return lax.ppermute(shard, axis, pairs)


def basis_integral(member, count_points, start_point, end_point):
    poly_terms = [1.0]
    denominator = 1.0
    for partner in range(count_points):
        if partner != member:
            widened = [0.0] * (len(poly_terms) + 1)
            for degree in range(len(poly_terms)):
                widened[degree + 1] += poly_terms[degree]
                widened[degree] -= partner * poly_terms[degree]
            poly_terms = widened
            denominator = denominator * (member - partner)
    integral = 0.0
    for degree in range(len(poly_terms)):
        integral += (
            poly_terms[degree]
            * (end_point ** (degree + 1) - start_point ** (degree + 1))
            / (degree + 1)
        )
    return integral / denominator


def quadrature_rows(count_steps):
    weights = [[0.0] * (count_steps + 1) for interval in range(count_steps)]
    for interval in range(count_steps):
        for member in range(interval + 2):
            weights[interval][member] = basis_integral(
                member, interval + 2, 1.0 * interval, 1.0 * interval + 1.0
            )
        weights[interval][interval] -= 1.0
    return weights


def extend(concentration):
    return padded_2(concentration, (("gx", 0), ("gy", 1)), 2)


def face_table(mobility):
    padded = padded_2(mobility, (("gx", 0), ("gy", 1)), 1)
    centre = padded[1:-1, 1:-1]
    x_plus = 0.5 * (centre + padded[2:, 1:-1])
    x_minus = 0.5 * (centre + padded[:-2, 1:-1])
    y_plus = 0.5 * (centre + padded[1:-1, 2:])
    y_minus = 0.5 * (centre + padded[1:-1, :-2])
    z_plus = 0.5 * (centre + jnp.roll(centre, -1, 2))
    z_minus = 0.5 * (centre + jnp.roll(centre, 1, 2))
    return (x_plus, x_minus, y_plus, y_minus, z_plus, z_minus)


def tendency_local(padded, faces):
    centre = padded[1:-1, 1:-1]
    laplace = -6.0 * centre
    laplace = laplace + padded[2:, 1:-1] + padded[:-2, 1:-1]
    laplace = laplace + padded[1:-1, 2:] + padded[1:-1, :-2]
    laplace = laplace + jnp.roll(centre, 1, 2) + jnp.roll(centre, -1, 2)
    potential = centre * centre * centre - centre - gradient_energy * laplace
    inner = potential[1:-1, 1:-1]
    result = faces[0] * (potential[2:, 1:-1] - inner) - faces[1] * (inner - potential[:-2, 1:-1])
    result = (
        result
        + faces[2] * (potential[1:-1, 2:] - inner)
        - faces[3] * (inner - potential[1:-1, :-2])
    )
    result = (
        result
        + faces[4] * (jnp.roll(inner, -1, 2) - inner)
        - faces[5] * (inner - jnp.roll(inner, 1, 2))
    )
    return result


def weighted_sum(weight_row, history):
    total = jnp.zeros(history.shape[1:], jnp.float32)
    for member in range(history.shape[0]):
        total = total + weight_row[member] * history[member]
    return total


def body(initial, mobility):
    level_count = lax.axis_size("level")
    level_id = lax.axis_index("level")
    faces = face_table(mobility)
    coefficients = jnp.asarray(quadrature_rows(STEPS), jnp.float32)
    node_ids = jnp.arange(STEPS + 1, dtype=jnp.int32)[:, None, None, None]
    solution = initial
    history = jnp.zeros((STEPS + 1,) + initial.shape, jnp.float32)
    for wave in range(STEPS + level_count - 1):
        interval = wave - level_id
        current = tendency_local(extend(solution), faces)
        arrived = passed_along(current, "level", 1)
        history = jnp.where(node_ids == interval + 1, arrived[None], history)
        weight_row = coefficients[jnp.clip(interval, 0, STEPS - 1)]
        correction = weighted_sum(weight_row, history)
        correction = jnp.where(level_id > 0, correction, jnp.zeros_like(correction))
        stepped = solution + time_step * (current + correction)
        active = jnp.logical_and(interval >= 0, interval < STEPS)
        solution = jnp.where(active, stepped, solution)
    return solution[None]


def window_kernel(weights, c_ref, m_ref, out_ref, raw, c0, mx, my, mz, rates_a, rates_b, sol_a, sol_b,
                  ready, finals, stage, send_sem, recv_sem, fwd_send_sem, fwd_recv_sem, own_sem,
                  fin_send_sem, fin_recv_sem, fin_own_sem):
    steps = len(weights)
    level = lax.axis_index("level")
    gx = lax.axis_index("gx")
    gy = lax.axis_index("gy")
    count_y = lax.axis_size("gy")
    x = level // 2
    core = level % 2
    tile = 2 * gx + x
    above = lax.rem(gy + 1, count_y)
    below = lax.rem(gy + count_y - 1, count_y)
    mesh_type = pl.DeviceIdType.MESH

    barrier = pltpu.get_barrier_semaphore()
    greeted = [(level + 1 - 2 * core, gx, gy)]
    greeted += [(2 * (1 - x) + core, gx, gy), (2 * (1 - x) + core, 1 - gx, gy), (level, 1 - gx, gy)]
    greeted += [(level, side, other) for side in (gx, 1 - gx) for other in (above, below)]
    for device in greeted:
        pl.semaphore_signal(barrier, inc=1, device_id=device, device_id_type=mesh_type)
    def aligned(row):
        return pl.multiple_of(row, 8)

    def region(array, half, row, count):
        return raw.at[array, pl.ds(4 * half, 4), pl.ds(aligned(row), count), :]

    def outgoing(array, source):
        partner_tile = 2 * (1 - gx) + x
        low = jnp.where(partner_tile == 3, 1, 0)

        def piece(row, count):
            return source.at[:, pl.ds(aligned(row), count), :]

        def copy(src, dst, slot, kind, device):
            return pltpu.make_async_remote_copy(
                src_ref=src, dst_ref=dst, send_sem=send_sem.at[slot], recv_sem=recv_sem.at[kind],
                device_id=device, device_id_type=mesh_type)

        to_above = (level, 0, above)
        to_below = (level, 1, below)
        partner = (level, 1 - gx, gy)
        row_to = 8 * jnp.maximum(2 - partner_tile, 0)
        return [
            (None, copy(piece(8 * low, 24), region(array, gx, row_to, 24), 0, 0, partner)),
            (x == gx, copy(piece(24, 8), region(array, gx, jnp.where(x == gx, 8 * (5 - partner_tile), 0), 8), 1, 1, partner)),
            (x == 0, copy(piece(16, 16), region(array, gx, 0, 16), 2, 2 + gx, to_above)),
            (x == 1, copy(piece(24, 8), region(array, gx, 0, 8), 2, 2 + gx, to_above)),
            (x == 1, copy(piece(0, 16), region(array, gx, 24, 16), 3, 3 - gx, to_below)),
            (x == 0, copy(piece(0, 8), region(array, gx, 32, 8), 3, 3 - gx, to_below)),
        ]

    def when(condition, action):
        if condition is None:
            action()
        else:
            pl.when(condition)(action)

    sibling = (level + 1 - 2 * core, gx, gy)

    def arriving(array):
        def copy(half, row, count, kind):
            where = region(array, half, row, count)
            landed = pltpu.make_async_remote_copy(
                src_ref=where, dst_ref=where, send_sem=send_sem.at[0], recv_sem=recv_sem.at[kind],
                device_id=sibling, device_id_type=mesh_type)
            handed = pltpu.make_async_remote_copy(
                src_ref=where, dst_ref=where, send_sem=fwd_send_sem.at[kind],
                recv_sem=fwd_recv_sem.at[kind], device_id=sibling, device_id_type=mesh_type)
            return landed, handed

        same = x == gx
        entries = [
            (None, copy(1 - gx, 8 * jnp.maximum(2 - tile, 0), 24, 0)),
            (jnp.logical_not(same), copy(1 - gx, jnp.where(same, 0, 8 * (5 - tile)), 8, 1)),
        ]
        for half, kind in ((gx, 2), (1 - gx, 3)):
            entries.append((same, copy(half, 24 * gx, 16, kind)))
            entries.append((jnp.logical_not(same), copy(half, 32 * gx, 8, kind)))
        return entries

    def own(array, source):
        low = jnp.where(tile == 3, 1, 0)
        row_to = 8 * jnp.maximum(2 - tile, 0)
        return [
            (None, pltpu.make_async_copy(
                source.at[:, pl.ds(aligned(8 * low), 24), :], region(array, gx, row_to, 24), own_sem.at[array, 0])),
            (x != gx, pltpu.make_async_copy(
                source.at[:, pl.ds(24, 8), :], region(array, gx, jnp.where(x != gx, 8 * (5 - tile), 0), 8),
                own_sem.at[array, 1])),
        ]

    width = c_ref.shape[2]
    parts = width // 128

    def one_hot(inverse):
        natural = lax.broadcasted_iota(jnp.int32, (width, width), 1 if inverse else 0)
        placed = lax.broadcasted_iota(jnp.int32, (width, width), 0 if inverse else 1)
        hit = natural == parts * lax.rem(placed, 128) + placed // 128
        return jnp.where(hit, 1.0, 0.0).astype(jnp.bfloat16)

    def moved(cells, matrix):
        high = cells.astype(jnp.bfloat16)
        rest = cells - high.astype(jnp.float32)
        middle = rest.astype(jnp.bfloat16)
        low = (rest - middle.astype(jnp.float32)).astype(jnp.bfloat16)
        taken = [jnp.dot(part, matrix, preferred_element_type=jnp.float32) for part in (high, middle, low)]
        return (taken[0] + taken[1]) + taken[2]

    def interleave(array, source):
        matrix = one_hot(False)
        for layer in range(4):
            stage[array, layer] = moved(source[layer], matrix)

    for array, source in enumerate((c_ref, m_ref)):
        pl.when(core == array)(functools.partial(interleave, array, source))
    pl.semaphore_wait(barrier, len(greeted))
    for array in range(2):
        @pl.when(core == array)
        def _(array=array):
            for condition, copy in outgoing(array, stage.at[array]):
                when(condition, copy.start)
    for array, source in enumerate((c_ref, m_ref)):
        pl.when(core != array)(functools.partial(interleave, array, source))
    staged = (stage.at[0], stage.at[1])
    for array, source in enumerate(staged):
        for condition, copy in own(array, source):
            when(condition, copy.start)
    for array in range(2):
        @pl.when(core == array)
        def _(array=array):
            for condition, (landed, handed) in arriving(array):
                def pass_on(landed=landed, handed=handed):
                    landed.wait_recv()
                    handed.start()
                when(condition, pass_on)
    for array, source in enumerate(staged):
        for condition, copy in own(array, source):
            when(condition, copy.wait)
    for array, source in enumerate(staged):
        @pl.when(core == array)
        def _(array=array, source=source):
            for condition, copy in outgoing(array, source):
                when(condition, copy.wait_send)
            for condition, (landed, handed) in arriving(array):
                when(condition, handed.wait_send)
            for condition, (landed, handed) in arriving(1 - array):
                when(condition, handed.wait_recv)

    def roll_x(cells, by):
        return pltpu.roll(cells, by % 8, 0)

    def roll_z(cells, by):
        pieces = [cells[:, 128 * part:128 * part + 128] for part in range(parts)]
        if by < 0:
            pieces = pieces[1:] + [pltpu.roll(pieces[0], 127, 1)]
        else:
            pieces = [pltpu.roll(pieces[-1], 1, 1)] + pieces[:-1]
        return jnp.concatenate(pieces, axis=1)

    def turn(block, carry):
        row = pl.multiple_of(8 * block, 8)
        for array, target in ((0, c0), (1, sol_a)):
            for lane in range(0, width, 128):
                cells = raw[array, :, pl.ds(row, 8), lane:lane + 128]
                target[pl.ds(row, 8), :, lane:lane + 128] = jnp.swapaxes(cells, 0, 1)
        return carry

    lax.fori_loop(0, 5, turn, 0)

    half_step = 0.5 * time_step

    def faces(row, carry):
        here = sol_a[row]
        mx[row] = half_step * (here + roll_x(here, -1))
        mz[row] = half_step * (here + roll_z(here, -1))
        my[row] = half_step * (here + sol_a[row + 1])
        return carry

    lax.fori_loop(1, 39, faces, 0)

    def potential(state, row):
        centre = state[row]
        around = state[row - 1] + state[row + 1]
        around = around + (roll_x(centre, 1) + roll_x(centre, -1))
        around = around + (roll_z(centre, 1) + roll_z(centre, -1))
        return (centre * centre + (6.0 * gradient_energy - 1.0)) * centre - gradient_energy * around

    def evaluate(state, reach, rates_out, update):
        first, last = 16 - reach, 24 + reach
        size = max(count for count in range(4, 17) if (last - first) % count == 0)
        here = potential(state, first)
        flux = my[first - 1] * (here - potential(state, first - 1))

        def group(index, carry):
            here, flux = carry
            for offset in range(size):
                row = first + size * index + offset
                after = potential(state, row + 1)
                flux_after = my[row] * (after - here)
                flux_x = mx[row] * (roll_x(here, -1) - here)
                flux_z = mz[row] * (roll_z(here, -1) - here)
                rate = flux_after - flux
                rate = rate + (flux_x - roll_x(flux_x, 1))
                rate = rate + (flux_z - roll_z(flux_z, 1))
                if rates_out is not None:
                    rates_out[row] = rate
                if update is not None:
                    update(row, rate)
                here, flux = after, flux_after
            return here, flux

        lax.fori_loop(0, (last - first) // size, group, (here, flux))

    def deliveries(slot):
        result = []
        into = finals.at[:, pl.ds(aligned(8 * tile), 8), :]
        for to_x, to_gx in ((slot, 0), (slot, 1)):
            stays = jnp.logical_and(x == to_x, gx == to_gx)
            out = ready.at[slot, pl.ds(4 * to_gx, 4)]
            remote = pltpu.make_async_remote_copy(
                src_ref=out, dst_ref=into, send_sem=fin_send_sem.at[2 * slot + to_gx],
                recv_sem=fin_recv_sem.at[tile], device_id=(2 * to_x + core, to_gx, gy),
                device_id_type=mesh_type)
            local = pltpu.make_async_copy(out, into, fin_own_sem)
            result.append((pl.when(jnp.logical_not(stays)), remote, pl.when(stays), local))
        return result

    def send_out(slot, state):
        for lane in range(0, width, 128):
            ready[slot, :, :, lane:lane + 128] = jnp.swapaxes(state[16:24, :, lane:lane + 128], 0, 1)
        for goes, remote, stays, local in deliveries(slot):
            goes(remote.start)
            stays(local.start)

    first_reach = 2 * (steps + 2)

    def run_level(index):
        below_rates = (rates_a, rates_b)[(index + 1) % 2]
        own_rates = (rates_a, rates_b)[index % 2]
        states = (sol_a, sol_b)

        def below_rate(node, row):
            return rates_a[0, row] if node == 0 else below_rates[node, row]

        def corrected(interval, row, base, rate):
            total = rate
            if index > 0:
                for node in range(interval + 2):
                    factor = weights[interval][node]
                    if interval == 0 and node == 0:
                        factor = factor + 1.0
                        total = factor * below_rate(0, row)
                    else:
                        total = total + factor * below_rate(node, row)
            return base + total

        for interval in range(steps + 1):
            reach = first_reach - 2 * (index + interval)
            source = c0 if interval == 0 else states[interval % 2]
            target = states[(interval + 1) % 2]

            def update(row, rate, interval=interval, source=source, target=target):
                target[row] = corrected(interval, row, source[row], rate)

            if interval == 0 and index > 0:
                def start(group, carry, update=update, reach=reach):
                    for offset in range(4):
                        update(16 - reach + 4 * group + offset, None)
                    return carry
                lax.fori_loop(0, (8 + 2 * reach) // 4, start, 0)
            elif interval < steps:
                evaluate(source, reach, own_rates.at[interval] if index < 3 else None, update)
            elif index < 3:
                evaluate(source, reach, own_rates.at[interval], None)
            if interval == steps - 1:
                @pl.when(core == index % 2)
                def _(target=target):
                    send_out(index // 2, target)

    for index in range(3):
        run_level(index)
    pl.when(core == 1)(lambda: run_level(3))

    for slot in range(2):
        for goes, remote, stays, local in deliveries(slot):
            goes(remote.wait_send)
            stays(local.wait)
    for source_tile in range(4):
        into = finals.at[:, pl.ds(8 * source_tile, 8), :]
        arrived = pltpu.make_async_remote_copy(
            src_ref=into, dst_ref=into, send_sem=fin_send_sem.at[0],
            recv_sem=fin_recv_sem.at[source_tile], device_id=sibling, device_id_type=mesh_type)
        pl.when(tile != source_tile)(arrived.wait_recv)
    matrix = one_hot(True)
    for layer in range(4):
        out_ref[0, layer] = moved(finals[layer], matrix)


def window_body(initial, mobility):
    f32 = jnp.float32
    width = initial.shape[2]
    weights = quadrature_rows(STEPS)
    field = pltpu.VMEM((40, 8, width), f32)
    return pl.pallas_call(
        functools.partial(window_kernel, weights),
        out_shape=jax.ShapeDtypeStruct((1,) + initial.shape, f32),
        in_specs=[pl.BlockSpec(memory_space=pltpu.VMEM)] * 2,
        out_specs=pl.BlockSpec(memory_space=pltpu.VMEM),
        scratch_shapes=[
            pltpu.VMEM((2, 8, 40, width), f32),
            field, field, field, field,
            pltpu.VMEM((STEPS + 1, 40, 8, width), f32),
            pltpu.VMEM((STEPS + 1, 40, 8, width), f32),
            field, field,
            pltpu.VMEM((2, 8, 8, width), f32),
            pltpu.VMEM(initial.shape, f32),
            pltpu.VMEM((2,) + initial.shape, f32),
            pltpu.SemaphoreType.DMA((4,)),
            pltpu.SemaphoreType.DMA((4,)),
            pltpu.SemaphoreType.DMA((4,)),
            pltpu.SemaphoreType.DMA((4,)),
            pltpu.SemaphoreType.DMA((2, 2)),
            pltpu.SemaphoreType.DMA((4,)),
            pltpu.SemaphoreType.DMA((4,)),
            pltpu.SemaphoreType.DMA,
        ],
        compiler_params=pltpu.CompilerParams(
            collective_id=0, has_side_effects=True, vmem_limit_bytes=40 * 1024 * 1024
        ),
    )(initial, mobility)


def solution(mesh):
    placed = (P("gx", "gy", None), P("gx", "gy", None))

    def chosen(initial, mobility):
        sizes = mesh.shape
        whole = (sizes["level"], sizes["gx"]) == (4, 2) and initial.shape[:2] == (4, 32)
        if whole and sizes["gy"] > 1 and initial.shape[2] % 128 == 0:
            return window_body(initial, mobility)
        return body(initial, mobility)

    return jax.shard_map(
        chosen, mesh=mesh, in_specs=placed, out_specs=P("level", "gx", "gy", None), check_vma=False
    )
```

```python
import functools

import jax
import jax.numpy as jnp
from jax import lax
from jax.experimental import pallas as pl
from jax.experimental.pallas import tpu as pltpu
from jax.sharding import PartitionSpec as P

STEPS = 5


time_step = 0.004
gradient_energy = 1.0


def padded_2(cells, sides, width):
    for axis, dim in sides:
        count = lax.axis_size(axis)
        head = lax.slice_in_dim(cells, 0, width, axis=dim)
        tail = lax.slice_in_dim(cells, cells.shape[dim] - width, cells.shape[dim], axis=dim)
        cells = jnp.concatenate(
            [
                lax.ppermute(tail, axis, [(i, (i + 1) % count) for i in range(count)]),
                cells,
                lax.ppermute(head, axis, [((i + 1) % count, i) for i in range(count)]),
            ],
            axis=dim,
        )
    return cells


def passed_along(shard, axis, by):
    count = lax.axis_size(axis)
    pairs = [(i, i + by) for i in range(count) if 0 <= i + by < count]
    return lax.ppermute(shard, axis, pairs)


def basis_integral(member, count_points, start_point, end_point):
    poly_terms = [1.0]
    denominator = 1.0
    for partner in range(count_points):
        if partner != member:
            widened = [0.0] * (len(poly_terms) + 1)
            for degree in range(len(poly_terms)):
                widened[degree + 1] += poly_terms[degree]
                widened[degree] -= partner * poly_terms[degree]
            poly_terms = widened
            denominator = denominator * (member - partner)
    integral = 0.0
    for degree in range(len(poly_terms)):
        integral += (
            poly_terms[degree]
            * (end_point ** (degree + 1) - start_point ** (degree + 1))
            / (degree + 1)
        )
    return integral / denominator


def quadrature_rows(count_steps):
    weights = [[0.0] * (count_steps + 1) for interval in range(count_steps)]
    for interval in range(count_steps):
        for member in range(interval + 2):
            weights[interval][member] = basis_integral(
                member, interval + 2, 1.0 * interval, 1.0 * interval + 1.0
            )
        weights[interval][interval] -= 1.0
    return weights


def extend(concentration):
    return padded_2(concentration, (("gx", 0), ("gy", 1)), 2)


def face_table(mobility):
    padded = padded_2(mobility, (("gx", 0), ("gy", 1)), 1)
    centre = padded[1:-1, 1:-1]
    x_plus = 0.5 * (centre + padded[2:, 1:-1])
    x_minus = 0.5 * (centre + padded[:-2, 1:-1])
    y_plus = 0.5 * (centre + padded[1:-1, 2:])
    y_minus = 0.5 * (centre + padded[1:-1, :-2])
    z_plus = 0.5 * (centre + jnp.roll(centre, -1, 2))
    z_minus = 0.5 * (centre + jnp.roll(centre, 1, 2))
    return (x_plus, x_minus, y_plus, y_minus, z_plus, z_minus)


def tendency_local(padded, faces):
    centre = padded[1:-1, 1:-1]
    laplace = -6.0 * centre
    laplace = laplace + padded[2:, 1:-1] + padded[:-2, 1:-1]
    laplace = laplace + padded[1:-1, 2:] + padded[1:-1, :-2]
    laplace = laplace + jnp.roll(centre, 1, 2) + jnp.roll(centre, -1, 2)
    potential = centre * centre * centre - centre - gradient_energy * laplace
    inner = potential[1:-1, 1:-1]
    result = faces[0] * (potential[2:, 1:-1] - inner) - faces[1] * (inner - potential[:-2, 1:-1])
    result = (
        result
        + faces[2] * (potential[1:-1, 2:] - inner)
        - faces[3] * (inner - potential[1:-1, :-2])
    )
    result = (
        result
        + faces[4] * (jnp.roll(inner, -1, 2) - inner)
        - faces[5] * (inner - jnp.roll(inner, 1, 2))
    )
    return result


def weighted_sum(weight_row, history):
    total = jnp.zeros(history.shape[1:], jnp.float32)
    for member in range(history.shape[0]):
        total = total + weight_row[member] * history[member]
    return total


def body(initial, mobility):
    level_count = lax.axis_size("level")
    level_id = lax.axis_index("level")
    faces = face_table(mobility)
    coefficients = jnp.asarray(quadrature_rows(STEPS), jnp.float32)
    node_ids = jnp.arange(STEPS + 1, dtype=jnp.int32)[:, None, None, None]
    solution = initial
    history = jnp.zeros((STEPS + 1,) + initial.shape, jnp.float32)
    for wave in range(STEPS + level_count - 1):
        interval = wave - level_id
        current = tendency_local(extend(solution), faces)
        arrived = passed_along(current, "level", 1)
        history = jnp.where(node_ids == interval + 1, arrived[None], history)
        weight_row = coefficients[jnp.clip(interval, 0, STEPS - 1)]
        correction = weighted_sum(weight_row, history)
        correction = jnp.where(level_id > 0, correction, jnp.zeros_like(correction))
        stepped = solution + time_step * (current + correction)
        active = jnp.logical_and(interval >= 0, interval < STEPS)
        solution = jnp.where(active, stepped, solution)
    return solution[None]


def window_kernel(weights, c_ref, m_ref, out_ref, raw, c0, mx, my, mz, rates_a, rates_b, sol_a, sol_b,
                  ready, finals, stage, send_sem, recv_sem, fwd_send_sem, fwd_recv_sem, own_sem,
                  fin_send_sem, fin_recv_sem, fin_own_sem):
    steps = len(weights)
    level = lax.axis_index("level")
    gx = lax.axis_index("gx")
    gy = lax.axis_index("gy")
    count_y = lax.axis_size("gy")
    x = level // 2
    core = level % 2
    tile = 2 * gx + x
    above = lax.rem(gy + 1, count_y)
    below = lax.rem(gy + count_y - 1, count_y)
    mesh_type = pl.DeviceIdType.MESH

    barrier = pltpu.get_barrier_semaphore()
    greeted = [(level + 1 - 2 * core, gx, gy)]
    greeted += [(2 * (1 - x) + core, gx, gy), (2 * (1 - x) + core, 1 - gx, gy), (level, 1 - gx, gy)]
    greeted += [(level, side, other) for side in (gx, 1 - gx) for other in (above, below)]
    for device in greeted:
        pl.semaphore_signal(barrier, inc=1, device_id=device, device_id_type=mesh_type)
    def aligned(row):
        return pl.multiple_of(row, 8)

    def region(array, half, row, count):
        return raw.at[array, pl.ds(4 * half, 4), pl.ds(aligned(row), count), :]

    def outgoing(array, source):
        partner_tile = 2 * (1 - gx) + x
        low = jnp.where(partner_tile == 3, 1, 0)

        def piece(row, count):
            return source.at[:, pl.ds(aligned(row), count), :]

        def copy(src, dst, slot, kind, device):
            return pltpu.make_async_remote_copy(
                src_ref=src, dst_ref=dst, send_sem=send_sem.at[slot], recv_sem=recv_sem.at[kind],
                device_id=device, device_id_type=mesh_type)

        to_above = (level, 0, above)
        to_below = (level, 1, below)
        partner = (level, 1 - gx, gy)
        row_to = 8 * jnp.maximum(2 - partner_tile, 0)
        return [
            (None, copy(piece(8 * low, 8), region(array, gx, row_to, 8), 0, 0, partner)),
            (None, copy(piece(8 * low + 8, 8), region(array, gx, row_to + 8, 8), 4, 4, partner)),
            (None, copy(piece(8 * low + 16, 8), region(array, gx, row_to + 16, 8), 5, 5, partner)),
            (x == gx, copy(piece(24, 8), region(array, gx, jnp.where(x == gx, 8 * (5 - partner_tile), 0), 8), 1, 1, partner)),
            (x == 0, copy(piece(16, 16), region(array, gx, 0, 16), 2, 2 + gx, to_above)),
            (x == 1, copy(piece(24, 8), region(array, gx, 0, 8), 2, 2 + gx, to_above)),
            (x == 1, copy(piece(0, 16), region(array, gx, 24, 16), 3, 3 - gx, to_below)),
            (x == 0, copy(piece(0, 8), region(array, gx, 32, 8), 3, 3 - gx, to_below)),
        ]

    def when(condition, action):
        if condition is None:
            action()
        else:
            pl.when(condition)(action)

    sibling = (level + 1 - 2 * core, gx, gy)

    def arriving(array):
        def copy(half, row, count, kind):
            where = region(array, half, row, count)
            landed = pltpu.make_async_remote_copy(
                src_ref=where, dst_ref=where, send_sem=send_sem.at[0], recv_sem=recv_sem.at[kind],
                device_id=sibling, device_id_type=mesh_type)
            handed = pltpu.make_async_remote_copy(
                src_ref=where, dst_ref=where, send_sem=fwd_send_sem.at[kind],
                recv_sem=fwd_recv_sem.at[kind], device_id=sibling, device_id_type=mesh_type)
            return landed, handed

        same = x == gx
        entries = [
            (None, copy(1 - gx, 8 * jnp.maximum(2 - tile, 0), 8, 0)),
            (None, copy(1 - gx, 8 * jnp.maximum(2 - tile, 0) + 8, 8, 4)),
            (None, copy(1 - gx, 8 * jnp.maximum(2 - tile, 0) + 16, 8, 5)),
            (jnp.logical_not(same), copy(1 - gx, jnp.where(same, 0, 8 * (5 - tile)), 8, 1)),
        ]
        for half, kind in ((gx, 2), (1 - gx, 3)):
            entries.append((same, copy(half, 24 * gx, 16, kind)))
            entries.append((jnp.logical_not(same), copy(half, 32 * gx, 8, kind)))
        return entries

    def own(array, source):
        low = jnp.where(tile == 3, 1, 0)
        row_to = 8 * jnp.maximum(2 - tile, 0)
        return [
            (None, pltpu.make_async_copy(
                source.at[:, pl.ds(aligned(8 * low), 24), :], region(array, gx, row_to, 24), own_sem.at[array, 0])),
            (x != gx, pltpu.make_async_copy(
                source.at[:, pl.ds(24, 8), :], region(array, gx, jnp.where(x != gx, 8 * (5 - tile), 0), 8),
                own_sem.at[array, 1])),
        ]

    width = c_ref.shape[2]
    parts = width // 128

    def one_hot(inverse):
        natural = lax.broadcasted_iota(jnp.int32, (width, width), 1 if inverse else 0)
        placed = lax.broadcasted_iota(jnp.int32, (width, width), 0 if inverse else 1)
        hit = natural == parts * lax.rem(placed, 128) + placed // 128
        return jnp.where(hit, 1.0, 0.0).astype(jnp.bfloat16)

    def moved(cells, matrix):
        high = cells.astype(jnp.bfloat16)
        rest = cells - high.astype(jnp.float32)
        middle = rest.astype(jnp.bfloat16)
        low = (rest - middle.astype(jnp.float32)).astype(jnp.bfloat16)
        taken = [jnp.dot(part, matrix, preferred_element_type=jnp.float32) for part in (high, middle, low)]
        return (taken[0] + taken[1]) + taken[2]

    def interleave(array, source):
        matrix = one_hot(False)
        for layer in range(4):
            stage[array, layer] = moved(source[layer], matrix)

    for array, source in enumerate((c_ref, m_ref)):
        pl.when(core == array)(functools.partial(interleave, array, source))
    pl.semaphore_wait(barrier, len(greeted))
    for array in range(2):
        @pl.when(core == array)
        def _(array=array):
            for condition, copy in outgoing(array, stage.at[array]):
                when(condition, copy.start)
    for array, source in enumerate((c_ref, m_ref)):
        pl.when(core != array)(functools.partial(interleave, array, source))
    staged = (stage.at[0], stage.at[1])
    for array, source in enumerate(staged):
        for condition, copy in own(array, source):
            when(condition, copy.start)
    for array in range(2):
        @pl.when(core == array)
        def _(array=array):
            for condition, (landed, handed) in arriving(array):
                def pass_on(landed=landed, handed=handed):
                    landed.wait_recv()
                    handed.start()
                when(condition, pass_on)
    for array, source in enumerate(staged):
        for condition, copy in own(array, source):
            when(condition, copy.wait)
    for array, source in enumerate(staged):
        @pl.when(core == array)
        def _(array=array, source=source):
            for condition, copy in outgoing(array, source):
                when(condition, copy.wait_send)
            for condition, (landed, handed) in arriving(array):
                when(condition, handed.wait_send)
            for condition, (landed, handed) in arriving(1 - array):
                when(condition, handed.wait_recv)

    def roll_x(cells, by):
        return pltpu.roll(cells, by % 8, 0)

    def roll_z(cells, by):
        pieces = [cells[:, 128 * part:128 * part + 128] for part in range(parts)]
        if by < 0:
            pieces = pieces[1:] + [pltpu.roll(pieces[0], 127, 1)]
        else:
            pieces = [pltpu.roll(pieces[-1], 1, 1)] + pieces[:-1]
        return jnp.concatenate(pieces, axis=1)

    for row in range(0, 40, 8):
        for array, target in ((0, c0), (1, sol_a)):
            for lane in range(0, width, 128):
                cells = raw[array, :, row:row + 8, lane:lane + 128]
                target[row:row + 8, :, lane:lane + 128] = jnp.swapaxes(cells, 0, 1)

    half_step = 0.5 * time_step

    def faces(group, carry):
        for offset in range(19):
            row = 1 + 19 * group + offset
            here = sol_a[row]
            mx[row] = half_step * (here + roll_x(here, -1))
            mz[row] = half_step * (here + roll_z(here, -1))
            my[row] = half_step * (here + sol_a[row + 1])
        return carry

    lax.fori_loop(0, 2, faces, 0)

    def potential(state, row):
        centre = state[row]
        around = state[row - 1] + state[row + 1]
        around = around + (roll_x(centre, 1) + roll_x(centre, -1))
        around = around + (roll_z(centre, 1) + roll_z(centre, -1))
        return (centre * centre + (6.0 * gradient_energy - 1.0)) * centre - gradient_energy * around

    def evaluate(state, reach, rates_out, update):
        first, last = 16 - reach, 24 + reach
        size = max(count for count in range(4, 17) if (last - first) % count == 0)
        here = potential(state, first)
        flux = my[first - 1] * (here - potential(state, first - 1))

        def group(index, carry):
            here, flux = carry
            for offset in range(size):
                row = first + size * index + offset
                after = potential(state, row + 1)
                flux_after = my[row] * (after - here)
                flux_x = mx[row] * (roll_x(here, -1) - here)
                flux_z = mz[row] * (roll_z(here, -1) - here)
                rate = flux_after - flux
                rate = rate + (flux_x - roll_x(flux_x, 1))
                rate = rate + (flux_z - roll_z(flux_z, 1))
                if rates_out is not None:
                    rates_out[row] = rate
                if update is not None:
                    update(row, rate)
                here, flux = after, flux_after
            return here, flux

        lax.fori_loop(0, (last - first) // size, group, (here, flux))

    def deliveries(slot):
        result = []
        into = finals.at[:, pl.ds(aligned(8 * tile), 8), :]
        for to_x, to_gx in ((slot, 0), (slot, 1)):
            stays = jnp.logical_and(x == to_x, gx == to_gx)
            out = ready.at[slot, pl.ds(4 * to_gx, 4)]
            remote = pltpu.make_async_remote_copy(
                src_ref=out, dst_ref=into, send_sem=fin_send_sem.at[2 * slot + to_gx],
                recv_sem=fin_recv_sem.at[tile], device_id=(2 * to_x + core, to_gx, gy),
                device_id_type=mesh_type)
            local = pltpu.make_async_copy(out, into, fin_own_sem)
            result.append((pl.when(jnp.logical_not(stays)), remote, pl.when(stays), local))
        return result

    def send_out(slot, state):
        for lane in range(0, width, 128):
            ready[slot, :, :, lane:lane + 128] = jnp.swapaxes(state[16:24, :, lane:lane + 128], 0, 1)
        for goes, remote, stays, local in deliveries(slot):
            goes(remote.start)
            stays(local.start)

    first_reach = 2 * (steps + 2)

    def run_level(index):
        below_rates = (rates_a, rates_b)[(index + 1) % 2]
        own_rates = (rates_a, rates_b)[index % 2]
        states = (sol_a, sol_b)

        def below_rate(node, row):
            return rates_a[0, row] if node == 0 else below_rates[node, row]

        def corrected(interval, row, base, rate):
            total = rate
            if index > 0:
                for node in range(interval + 2):
                    factor = weights[interval][node]
                    if interval == 0 and node == 0:
                        factor = factor + 1.0
                        total = factor * below_rate(0, row)
                    else:
                        total = total + factor * below_rate(node, row)
            return base + total

        for interval in range(steps + 1):
            reach = first_reach - 2 * (index + interval)
            source = c0 if interval == 0 else states[interval % 2]
            target = states[(interval + 1) % 2]

            def update(row, rate, interval=interval, source=source, target=target):
                target[row] = corrected(interval, row, source[row], rate)

            if interval == 0 and index > 0:
                def start(group, carry, update=update, reach=reach):
                    for offset in range(4):
                        update(16 - reach + 4 * group + offset, None)
                    return carry
                lax.fori_loop(0, (8 + 2 * reach) // 4, start, 0)
            elif interval < steps:
                evaluate(source, reach, own_rates.at[interval] if index < 3 else None, update)
            elif index < 3:
                evaluate(source, reach, own_rates.at[interval], None)
            if interval == steps - 1:
                @pl.when(core == index % 2)
                def _(target=target):
                    send_out(index // 2, target)

    for index in range(3):
        run_level(index)
    pl.when(core == 1)(lambda: run_level(3))

    for slot in range(2):
        for goes, remote, stays, local in deliveries(slot):
            goes(remote.wait_send)
            stays(local.wait)
    for source_tile in range(4):
        into = finals.at[:, pl.ds(8 * source_tile, 8), :]
        arrived = pltpu.make_async_remote_copy(
            src_ref=into, dst_ref=into, send_sem=fin_send_sem.at[0],
            recv_sem=fin_recv_sem.at[source_tile], device_id=sibling, device_id_type=mesh_type)
        pl.when(tile != source_tile)(arrived.wait_recv)
    matrix = one_hot(True)
    for layer in range(4):
        out_ref[0, layer] = moved(finals[layer], matrix)


def window_body(initial, mobility):
    f32 = jnp.float32
    width = initial.shape[2]
    weights = quadrature_rows(STEPS)
    field = pltpu.VMEM((40, 8, width), f32)
    return pl.pallas_call(
        functools.partial(window_kernel, weights),
        out_shape=jax.ShapeDtypeStruct((1,) + initial.shape, f32),
        in_specs=[pl.BlockSpec(memory_space=pltpu.VMEM)] * 2,
        out_specs=pl.BlockSpec(memory_space=pltpu.VMEM),
        scratch_shapes=[
            pltpu.VMEM((2, 8, 40, width), f32),
            field, field, field, field,
            pltpu.VMEM((STEPS + 1, 40, 8, width), f32),
            pltpu.VMEM((STEPS + 1, 40, 8, width), f32),
            field, field,
            pltpu.VMEM((2, 8, 8, width), f32),
            pltpu.VMEM(initial.shape, f32),
            pltpu.VMEM((2,) + initial.shape, f32),
            pltpu.SemaphoreType.DMA((6,)),
            pltpu.SemaphoreType.DMA((6,)),
            pltpu.SemaphoreType.DMA((6,)),
            pltpu.SemaphoreType.DMA((6,)),
            pltpu.SemaphoreType.DMA((2, 2)),
            pltpu.SemaphoreType.DMA((4,)),
            pltpu.SemaphoreType.DMA((4,)),
            pltpu.SemaphoreType.DMA,
        ],
        compiler_params=pltpu.CompilerParams(
            collective_id=0, has_side_effects=True, vmem_limit_bytes=40 * 1024 * 1024
        ),
    )(initial, mobility)


def solution(mesh):
    placed = (P("gx", "gy", None), P("gx", "gy", None))

    def chosen(initial, mobility):
        sizes = mesh.shape
        whole = (sizes["level"], sizes["gx"]) == (4, 2) and initial.shape[:2] == (4, 32)
        if whole and sizes["gy"] > 1 and initial.shape[2] % 128 == 0:
            return window_body(initial, mobility)
        return body(initial, mobility)

    return jax.shard_map(
        chosen, mesh=mesh, in_specs=placed, out_specs=P("level", "gx", "gy", None), check_vma=False
    )
```

```python
import functools

import jax
import jax.numpy as jnp
from jax import lax
from jax.experimental import pallas as pl
from jax.experimental.pallas import tpu as pltpu
from jax.sharding import PartitionSpec as P

STEPS = 5


time_step = 0.004
gradient_energy = 1.0


def padded_2(cells, sides, width):
    for axis, dim in sides:
        count = lax.axis_size(axis)
        head = lax.slice_in_dim(cells, 0, width, axis=dim)
        tail = lax.slice_in_dim(cells, cells.shape[dim] - width, cells.shape[dim], axis=dim)
        cells = jnp.concatenate(
            [
                lax.ppermute(tail, axis, [(i, (i + 1) % count) for i in range(count)]),
                cells,
                lax.ppermute(head, axis, [((i + 1) % count, i) for i in range(count)]),
            ],
            axis=dim,
        )
    return cells


def passed_along(shard, axis, by):
    count = lax.axis_size(axis)
    pairs = [(i, i + by) for i in range(count) if 0 <= i + by < count]
    return lax.ppermute(shard, axis, pairs)


def basis_integral(member, count_points, start_point, end_point):
    poly_terms = [1.0]
    denominator = 1.0
    for partner in range(count_points):
        if partner != member:
            widened = [0.0] * (len(poly_terms) + 1)
            for degree in range(len(poly_terms)):
                widened[degree + 1] += poly_terms[degree]
                widened[degree] -= partner * poly_terms[degree]
            poly_terms = widened
            denominator = denominator * (member - partner)
    integral = 0.0
    for degree in range(len(poly_terms)):
        integral += (
            poly_terms[degree]
            * (end_point ** (degree + 1) - start_point ** (degree + 1))
            / (degree + 1)
        )
    return integral / denominator


def quadrature_rows(count_steps):
    weights = [[0.0] * (count_steps + 1) for interval in range(count_steps)]
    for interval in range(count_steps):
        for member in range(interval + 2):
            weights[interval][member] = basis_integral(
                member, interval + 2, 1.0 * interval, 1.0 * interval + 1.0
            )
        weights[interval][interval] -= 1.0
    return weights


def extend(concentration):
    return padded_2(concentration, (("gx", 0), ("gy", 1)), 2)


def face_table(mobility):
    padded = padded_2(mobility, (("gx", 0), ("gy", 1)), 1)
    centre = padded[1:-1, 1:-1]
    x_plus = 0.5 * (centre + padded[2:, 1:-1])
    x_minus = 0.5 * (centre + padded[:-2, 1:-1])
    y_plus = 0.5 * (centre + padded[1:-1, 2:])
    y_minus = 0.5 * (centre + padded[1:-1, :-2])
    z_plus = 0.5 * (centre + jnp.roll(centre, -1, 2))
    z_minus = 0.5 * (centre + jnp.roll(centre, 1, 2))
    return (x_plus, x_minus, y_plus, y_minus, z_plus, z_minus)


def tendency_local(padded, faces):
    centre = padded[1:-1, 1:-1]
    laplace = -6.0 * centre
    laplace = laplace + padded[2:, 1:-1] + padded[:-2, 1:-1]
    laplace = laplace + padded[1:-1, 2:] + padded[1:-1, :-2]
    laplace = laplace + jnp.roll(centre, 1, 2) + jnp.roll(centre, -1, 2)
    potential = centre * centre * centre - centre - gradient_energy * laplace
    inner = potential[1:-1, 1:-1]
    result = faces[0] * (potential[2:, 1:-1] - inner) - faces[1] * (inner - potential[:-2, 1:-1])
    result = (
        result
        + faces[2] * (potential[1:-1, 2:] - inner)
        - faces[3] * (inner - potential[1:-1, :-2])
    )
    result = (
        result
        + faces[4] * (jnp.roll(inner, -1, 2) - inner)
        - faces[5] * (inner - jnp.roll(inner, 1, 2))
    )
    return result


def weighted_sum(weight_row, history):
    total = jnp.zeros(history.shape[1:], jnp.float32)
    for member in range(history.shape[0]):
        total = total + weight_row[member] * history[member]
    return total


def body(initial, mobility):
    level_count = lax.axis_size("level")
    level_id = lax.axis_index("level")
    faces = face_table(mobility)
    coefficients = jnp.asarray(quadrature_rows(STEPS), jnp.float32)
    node_ids = jnp.arange(STEPS + 1, dtype=jnp.int32)[:, None, None, None]
    solution = initial
    history = jnp.zeros((STEPS + 1,) + initial.shape, jnp.float32)
    for wave in range(STEPS + level_count - 1):
        interval = wave - level_id
        current = tendency_local(extend(solution), faces)
        arrived = passed_along(current, "level", 1)
        history = jnp.where(node_ids == interval + 1, arrived[None], history)
        weight_row = coefficients[jnp.clip(interval, 0, STEPS - 1)]
        correction = weighted_sum(weight_row, history)
        correction = jnp.where(level_id > 0, correction, jnp.zeros_like(correction))
        stepped = solution + time_step * (current + correction)
        active = jnp.logical_and(interval >= 0, interval < STEPS)
        solution = jnp.where(active, stepped, solution)
    return solution[None]


def window_kernel(weights, c_hbm, m_hbm, out_ref, fields, in_sem, raw, c0, mx, my, mz, rates_a, rates_b, sol_a, sol_b,
                  ready, finals, stage, send_sem, recv_sem, fwd_send_sem, fwd_recv_sem, own_sem,
                  fin_send_sem, fin_recv_sem, fin_own_sem):
    steps = len(weights)
    fetched = [
        pltpu.make_async_copy(source, fields.at[array], in_sem.at[array])
        for array, source in enumerate((c_hbm, m_hbm))
    ]
    for copy in fetched:
        copy.start()
    level = lax.axis_index("level")
    gx = lax.axis_index("gx")
    gy = lax.axis_index("gy")
    count_y = lax.axis_size("gy")
    x = level // 2
    core = level % 2
    tile = 2 * gx + x
    above = lax.rem(gy + 1, count_y)
    below = lax.rem(gy + count_y - 1, count_y)
    mesh_type = pl.DeviceIdType.MESH

    barrier = pltpu.get_barrier_semaphore()
    greeted = [(level + 1 - 2 * core, gx, gy)]
    greeted += [(2 * (1 - x) + core, gx, gy), (2 * (1 - x) + core, 1 - gx, gy), (level, 1 - gx, gy)]
    greeted += [(level, side, other) for side in (gx, 1 - gx) for other in (above, below)]
    for device in greeted:
        pl.semaphore_signal(barrier, inc=1, device_id=device, device_id_type=mesh_type)
    def aligned(row):
        return pl.multiple_of(row, 8)

    def region(array, half, row, count):
        return raw.at[array, pl.ds(4 * half, 4), pl.ds(aligned(row), count), :]

    def outgoing(array, source):
        partner_tile = 2 * (1 - gx) + x
        low = jnp.where(partner_tile == 3, 1, 0)

        def piece(row, count):
            return source.at[:, pl.ds(aligned(row), count), :]

        def copy(src, dst, slot, kind, device):
            return pltpu.make_async_remote_copy(
                src_ref=src, dst_ref=dst, send_sem=send_sem.at[slot], recv_sem=recv_sem.at[kind],
                device_id=device, device_id_type=mesh_type)

        to_above = (level, 0, above)
        to_below = (level, 1, below)
        partner = (level, 1 - gx, gy)
        row_to = 8 * jnp.maximum(2 - partner_tile, 0)
        return [
            (None, copy(piece(8 * low, 8), region(array, gx, row_to, 8), 0, 0, partner)),
            (None, copy(piece(8 * low + 8, 8), region(array, gx, row_to + 8, 8), 4, 4, partner)),
            (None, copy(piece(8 * low + 16, 8), region(array, gx, row_to + 16, 8), 5, 5, partner)),
            (x == gx, copy(piece(24, 8), region(array, gx, jnp.where(x == gx, 8 * (5 - partner_tile), 0), 8), 1, 1, partner)),
            (x == 0, copy(piece(16, 16), region(array, gx, 0, 16), 2, 2 + gx, to_above)),
            (x == 1, copy(piece(24, 8), region(array, gx, 0, 8), 2, 2 + gx, to_above)),
            (x == 1, copy(piece(0, 16), region(array, gx, 24, 16), 3, 3 - gx, to_below)),
            (x == 0, copy(piece(0, 8), region(array, gx, 32, 8), 3, 3 - gx, to_below)),
        ]

    def when(condition, action):
        if condition is None:
            action()
        else:
            pl.when(condition)(action)

    sibling = (level + 1 - 2 * core, gx, gy)

    def arriving(array):
        def copy(half, row, count, kind):
            where = region(array, half, row, count)
            landed = pltpu.make_async_remote_copy(
                src_ref=where, dst_ref=where, send_sem=send_sem.at[0], recv_sem=recv_sem.at[kind],
                device_id=sibling, device_id_type=mesh_type)
            handed = pltpu.make_async_remote_copy(
                src_ref=where, dst_ref=where, send_sem=fwd_send_sem.at[kind],
                recv_sem=fwd_recv_sem.at[kind], device_id=sibling, device_id_type=mesh_type)
            return landed, handed

        same = x == gx
        entries = [
            (None, copy(1 - gx, 8 * jnp.maximum(2 - tile, 0), 8, 0)),
            (None, copy(1 - gx, 8 * jnp.maximum(2 - tile, 0) + 8, 8, 4)),
            (None, copy(1 - gx, 8 * jnp.maximum(2 - tile, 0) + 16, 8, 5)),
            (jnp.logical_not(same), copy(1 - gx, jnp.where(same, 0, 8 * (5 - tile)), 8, 1)),
        ]
        for half, kind in ((gx, 2), (1 - gx, 3)):
            entries.append((same, copy(half, 24 * gx, 16, kind)))
            entries.append((jnp.logical_not(same), copy(half, 32 * gx, 8, kind)))
        return entries

    def own(array, source):
        low = jnp.where(tile == 3, 1, 0)
        row_to = 8 * jnp.maximum(2 - tile, 0)
        return [
            (None, pltpu.make_async_copy(
                source.at[:, pl.ds(aligned(8 * low), 24), :], region(array, gx, row_to, 24), own_sem.at[array, 0])),
            (x != gx, pltpu.make_async_copy(
                source.at[:, pl.ds(24, 8), :], region(array, gx, jnp.where(x != gx, 8 * (5 - tile), 0), 8),
                own_sem.at[array, 1])),
        ]

    width = c_hbm.shape[2]
    parts = width // 128

    def one_hot(inverse):
        natural = lax.broadcasted_iota(jnp.int32, (width, width), 1 if inverse else 0)
        placed = lax.broadcasted_iota(jnp.int32, (width, width), 0 if inverse else 1)
        hit = natural == parts * lax.rem(placed, 128) + placed // 128
        return jnp.where(hit, 1.0, 0.0).astype(jnp.bfloat16)

    def moved(cells, matrix):
        high = cells.astype(jnp.bfloat16)
        rest = cells - high.astype(jnp.float32)
        middle = rest.astype(jnp.bfloat16)
        low = (rest - middle.astype(jnp.float32)).astype(jnp.bfloat16)
        taken = [jnp.dot(part, matrix, preferred_element_type=jnp.float32) for part in (high, middle, low)]
        return (taken[0] + taken[1]) + taken[2]

    matrix_in = one_hot(False)

    def interleave(array):
        fetched[array].wait()
        for layer in range(4):
            stage[array, layer] = moved(fields[array, layer], matrix_in)

    for array in range(2):
        pl.when(core == array)(functools.partial(interleave, array))
    pl.semaphore_wait(barrier, len(greeted))
    for array in range(2):
        @pl.when(core == array)
        def _(array=array):
            for condition, copy in outgoing(array, stage.at[array]):
                when(condition, copy.start)
    for array in range(2):
        pl.when(core != array)(functools.partial(interleave, array))
    staged = (stage.at[0], stage.at[1])
    for array, source in enumerate(staged):
        for condition, copy in own(array, source):
            when(condition, copy.start)
    for array in range(2):
        @pl.when(core == array)
        def _(array=array):
            for condition, (landed, handed) in arriving(array):
                def pass_on(landed=landed, handed=handed):
                    landed.wait_recv()
                    handed.start()
                when(condition, pass_on)
    for array, source in enumerate(staged):
        for condition, copy in own(array, source):
            when(condition, copy.wait)
    for array, source in enumerate(staged):
        @pl.when(core == array)
        def _(array=array, source=source):
            for condition, copy in outgoing(array, source):
                when(condition, copy.wait_send)
            for condition, (landed, handed) in arriving(array):
                when(condition, handed.wait_send)
            for condition, (landed, handed) in arriving(1 - array):
                when(condition, handed.wait_recv)

    def roll_x(cells, by):
        return pltpu.roll(cells, by % 8, 0)

    def roll_z(cells, by):
        pieces = [cells[:, 128 * part:128 * part + 128] for part in range(parts)]
        if by < 0:
            pieces = pieces[1:] + [pltpu.roll(pieces[0], 127, 1)]
        else:
            pieces = [pltpu.roll(pieces[-1], 1, 1)] + pieces[:-1]
        return jnp.concatenate(pieces, axis=1)

    for row in range(0, 40, 8):
        for array, target in ((0, c0), (1, sol_a)):
            for lane in range(0, width, 128):
                cells = raw[array, :, row:row + 8, lane:lane + 128]
                target[row:row + 8, :, lane:lane + 128] = jnp.swapaxes(cells, 0, 1)

    half_step = 0.5 * time_step

    def faces(group, carry):
        for offset in range(19):
            row = 1 + 19 * group + offset
            here = sol_a[row]
            mx[row] = half_step * (here + roll_x(here, -1))
            mz[row] = half_step * (here + roll_z(here, -1))
            my[row] = half_step * (here + sol_a[row + 1])
        return carry

    lax.fori_loop(0, 2, faces, 0)

    def potential(state, row):
        centre = state[row]
        around = state[row - 1] + state[row + 1]
        around = around + (roll_x(centre, 1) + roll_x(centre, -1))
        around = around + (roll_z(centre, 1) + roll_z(centre, -1))
        return (centre * centre + (6.0 * gradient_energy - 1.0)) * centre - gradient_energy * around

    def evaluate(state, reach, rates_out, update):
        first, last = 16 - reach, 24 + reach
        size = max(count for count in range(4, 17) if (last - first) % count == 0)
        here = potential(state, first)
        flux = my[first - 1] * (here - potential(state, first - 1))

        def group(index, carry):
            here, flux = carry
            for offset in range(size):
                row = first + size * index + offset
                after = potential(state, row + 1)
                flux_after = my[row] * (after - here)
                flux_x = mx[row] * (roll_x(here, -1) - here)
                flux_z = mz[row] * (roll_z(here, -1) - here)
                rate = flux_after - flux
                rate = rate + (flux_x - roll_x(flux_x, 1))
                rate = rate + (flux_z - roll_z(flux_z, 1))
                if rates_out is not None:
                    rates_out[row] = rate
                if update is not None:
                    update(row, rate)
                here, flux = after, flux_after
            return here, flux

        lax.fori_loop(0, (last - first) // size, group, (here, flux))

    def deliveries(slot):
        result = []
        into = finals.at[:, pl.ds(aligned(8 * tile), 8), :]
        for to_x, to_gx in ((slot, 0), (slot, 1)):
            stays = jnp.logical_and(x == to_x, gx == to_gx)
            out = ready.at[slot, pl.ds(4 * to_gx, 4)]
            remote = pltpu.make_async_remote_copy(
                src_ref=out, dst_ref=into, send_sem=fin_send_sem.at[2 * slot + to_gx],
                recv_sem=fin_recv_sem.at[tile], device_id=(2 * to_x + core, to_gx, gy),
                device_id_type=mesh_type)
            local = pltpu.make_async_copy(out, into, fin_own_sem)
            result.append((pl.when(jnp.logical_not(stays)), remote, pl.when(stays), local))
        return result

    def send_out(slot, state):
        for lane in range(0, width, 128):
            ready[slot, :, :, lane:lane + 128] = jnp.swapaxes(state[16:24, :, lane:lane + 128], 0, 1)
        for goes, remote, stays, local in deliveries(slot):
            goes(remote.start)
            stays(local.start)

    first_reach = 2 * (steps + 2)

    def run_level(index):
        below_rates = (rates_a, rates_b)[(index + 1) % 2]
        own_rates = (rates_a, rates_b)[index % 2]
        states = (sol_a, sol_b)

        def below_rate(node, row):
            return rates_a[0, row] if node == 0 else below_rates[node, row]

        def corrected(interval, row, base, rate):
            total = rate
            if index > 0:
                for node in range(interval + 2):
                    factor = weights[interval][node]
                    if interval == 0 and node == 0:
                        factor = factor + 1.0
                        total = factor * below_rate(0, row)
                    else:
                        total = total + factor * below_rate(node, row)
            return base + total

        for interval in range(steps + 1):
            reach = first_reach - 2 * (index + interval)
            source = c0 if interval == 0 else states[interval % 2]
            target = states[(interval + 1) % 2]

            def update(row, rate, interval=interval, source=source, target=target):
                target[row] = corrected(interval, row, source[row], rate)

            if interval == 0 and index > 0:
                def start(group, carry, update=update, reach=reach):
                    for offset in range(4):
                        update(16 - reach + 4 * group + offset, None)
                    return carry
                lax.fori_loop(0, (8 + 2 * reach) // 4, start, 0)
            elif interval < steps:
                evaluate(source, reach, own_rates.at[interval] if index < 3 else None, update)
            elif index < 3:
                evaluate(source, reach, own_rates.at[interval], None)
            if interval == steps - 1:
                @pl.when(core == index % 2)
                def _(target=target):
                    send_out(index // 2, target)

    for index in range(3):
        run_level(index)
    pl.when(core == 1)(lambda: run_level(3))

    for slot in range(2):
        for goes, remote, stays, local in deliveries(slot):
            goes(remote.wait_send)
            stays(local.wait)
    for source_tile in range(4):
        into = finals.at[:, pl.ds(8 * source_tile, 8), :]
        arrived = pltpu.make_async_remote_copy(
            src_ref=into, dst_ref=into, send_sem=fin_send_sem.at[0],
            recv_sem=fin_recv_sem.at[source_tile], device_id=sibling, device_id_type=mesh_type)
        pl.when(tile != source_tile)(arrived.wait_recv)
    matrix = one_hot(True)
    for layer in range(4):
        out_ref[0, layer] = moved(finals[layer], matrix)


def window_body(initial, mobility):
    f32 = jnp.float32
    width = initial.shape[2]
    weights = quadrature_rows(STEPS)
    field = pltpu.VMEM((40, 8, width), f32)
    return pl.pallas_call(
        functools.partial(window_kernel, weights),
        out_shape=jax.ShapeDtypeStruct((1,) + initial.shape, f32),
        in_specs=[pl.BlockSpec(memory_space=pltpu.HBM)] * 2,
        out_specs=pl.BlockSpec(memory_space=pltpu.VMEM),
        scratch_shapes=[
            pltpu.VMEM((2,) + initial.shape, f32),
            pltpu.SemaphoreType.DMA((2,)),
            pltpu.VMEM((2, 8, 40, width), f32),
            field, field, field, field,
            pltpu.VMEM((STEPS + 1, 40, 8, width), f32),
            pltpu.VMEM((STEPS + 1, 40, 8, width), f32),
            field, field,
            pltpu.VMEM((2, 8, 8, width), f32),
            pltpu.VMEM(initial.shape, f32),
            pltpu.VMEM((2,) + initial.shape, f32),
            pltpu.SemaphoreType.DMA((6,)),
            pltpu.SemaphoreType.DMA((6,)),
            pltpu.SemaphoreType.DMA((6,)),
            pltpu.SemaphoreType.DMA((6,)),
            pltpu.SemaphoreType.DMA((2, 2)),
            pltpu.SemaphoreType.DMA((4,)),
            pltpu.SemaphoreType.DMA((4,)),
            pltpu.SemaphoreType.DMA,
        ],
        compiler_params=pltpu.CompilerParams(
            collective_id=0, has_side_effects=True, vmem_limit_bytes=66322432
        ),
    )(initial, mobility)


def solution(mesh):
    placed = (P("gx", "gy", None), P("gx", "gy", None))

    def chosen(initial, mobility):
        sizes = mesh.shape
        whole = (sizes["level"], sizes["gx"]) == (4, 2) and initial.shape[:2] == (4, 32)
        if whole and sizes["gy"] > 1 and initial.shape[2] % 128 == 0:
            return window_body(initial, mobility)
        return body(initial, mobility)

    return jax.shard_map(
        chosen, mesh=mesh, in_specs=placed, out_specs=P("level", "gx", "gy", None), check_vma=False
    )
```
